32 devices in a mesh: px: 4 (over x, core), py: 8 (over z, y).
Axes of the slice: x: 2, y: 2, z: 4, core: 2. Of those that a mesh axis runs over, the one named last changes fastest.
Arguments:
- displacement: float32 [3, 131072], P(None, ('px', 'py')), may hold values from -6 to 6
- disp_prev: float32 [3, 131072], P(None, ('px', 'py')), may hold values from -6 to 6
- nodal_load: float32 [3, 131072], P(None, ('px', 'py')), may hold values from -6 to 6
- nodal_mass: float32 [131072], P(('px', 'py')), may hold values from 1 to 4
- modulus: float32 [16384], P(('px', 'py')), may hold values from 1 to 10
- stiffness: float32 [81, 81], replicated
- connectivity: int32 [27, 16384], P(None, ('px', 'py')), may hold values from 0 to 4607, as said below
- ghost_send: int32 [2, 8192], P(None, ('px', 'py')), may hold values from 0 to 4095
- contact_node: int32 [65536], P(('px', 'py')), may hold values from 0 to 4095
- contact_owner: int32 [65536], P(('px', 'py')), may hold values from 0 to 31, as said below
- pair_ids: int32 [2, 32768], P(None, ('px', 'py')), may hold values from 0 to 4095
- gap_start: float32 [3, 32768], P(None, ('px', 'py')), may hold values from -3 to 3
- penalty: float32 [32768], P(('px', 'py')), may hold values from 0.5 to 2
- friction: float32 [32768], P(('px', 'py')), may hold values from 0.2 to 0.6
- slip_state: int32 [3, 32768], P(None, ('px', 'py')), may hold values 0 or 1
Outputs:
- new_displacement: float32 [3, 131072], P(None, ('px', 'py'))
- acceleration: float32 [3, 131072], P(None, ('px', 'py'))
The draws below stay inside these ranges and needn't reach their ends.
Inputs may be any that keep to these rules, and one draw needn't show every extreme that they name: `connectivity`: of each device's 512 elements, the first 384 name only the device's own nodes, indices below 4096; the others name own and ghost nodes. `contact_owner`: among the 2048 contact nodes of one device at most 128 name the same owner; one owner is named by exactly 128 nodes of every device.
All inputs are finite; a program needn't handle non-finite values. No bound on the sum of `slip_state` on one device may be relied on, other than what follows from the above.
Results may differ from the reference program's by a relative error of at most 0.0003.
Values sent between devices are 32-bit elements; how exact they have to be, the bound alone decides.
A program may use at most 64 MiB of HBM per device.

```python
import math
import jax
import jax.numpy as jnp
from jax import lax

ELNODE = 27
ELDOF = 81
STEPS = 3
NODE_DEV = 4096
NE_DEV = 512
HB = 256
CN_DEV = 2048
PAIRS_PER_OWNER = 1024
NE_IN = 384
OWNER_TOTAL = 32
CAP = 128
NODES = 131072
ELEMS = 16384
GHOSTS = 8192
CONTACT = 65536
PAIRS = 32768


def draw_stiffness(key, part):
    key_coupling, key_diagonal = jax.random.split(key)
    random_part = jax.random.uniform(key_coupling, (ELDOF, ELDOF), jnp.float32, -1.0, 1.0)
    diagonal = jax.random.uniform(key_diagonal, (ELDOF,), jnp.float32, 1.2, 1.6)
    coupling = 0.06 * (random_part + random_part.T)
    identity = jnp.eye(ELDOF, dtype=jnp.float32)
    return 0.05 * (coupling * (1.0 - identity) + jnp.diag(diagonal))


def draw_connectivity(key, part):
    key_any, key_own = jax.random.split(key)
    anywhere = jax.random.randint(key_any, (ELNODE, OWNER_TOTAL, NE_DEV), 0, NODE_DEV + 2 * HB)
    own_only = jax.random.randint(key_own, (ELNODE, OWNER_TOTAL, NE_DEV), 0, NODE_DEV)
    column = jnp.arange(NE_DEV)[None, None, :]
    chosen = jnp.where(column < NE_IN, own_only, anywhere)
    return chosen.reshape(ELNODE, OWNER_TOTAL * NE_DEV).astype(jnp.int32)


def draw_contact_owner(key, part):
    key_star, key_pick, key_order = jax.random.split(key, 3)
    favored = jax.random.randint(key_star, (), 0, OWNER_TOTAL)
    total_slots = OWNER_TOTAL * CAP
    pick_keys = jax.random.split(key_pick, OWNER_TOTAL)
    order_keys = jax.random.split(key_order, OWNER_TOTAL)

    def one_device(pick_key, order_key):
        scores = jax.random.permutation(pick_key, total_slots)
        slot_owner = jnp.arange(total_slots) // CAP
        scores = scores + jnp.where(slot_owner == favored, total_slots, 0)
        top_values, chosen = lax.top_k(scores, CN_DEV)
        chosen = jax.random.permutation(order_key, chosen)
        return (chosen // CAP).astype(jnp.int32)
    return jax.vmap(one_device)(pick_keys, order_keys).reshape(OWNER_TOTAL * CN_DEV).astype(jnp.int32)


def with_ends(values, key, low, top_value):
    index_at = [jax.random.randint(jax.random.fold_in(key, axis), (), 0, length) for axis, length in enumerate(values.shape)]
    widest = values.shape.index(max(values.shape))
    neighbour = index_at[:widest] + [(index_at[widest] + 1) % values.shape[widest]] + index_at[widest + 1:]
    return values.at[tuple(index_at)].set(low).at[tuple(neighbour)].set(top_value)


def levels(own_key, extent, cuts, low, high):
    factor_of, own = 1.0, jax.random.fold_in(own_key, 6)
    for dim, blocks in cuts:
        steps = jnp.exp(jax.random.uniform(jax.random.fold_in(own, dim), (blocks,), jnp.float32, low / len(cuts), high / len(cuts)))
        factor_of = factor_of * jnp.repeat(steps, extent[dim] // blocks).reshape([-1 if axis == dim else 1 for axis in range(len(extent))])
    return factor_of


def normal_values(own_key, shape, deviation, most, shards=(), kind=jnp.bfloat16):
    gain = levels(own_key, shape, shards, -0.22, 0.18) if shards else 1.0
    values = jax.random.normal(own_key, shape, jnp.float32) * deviation * gain
    return jnp.minimum(jnp.maximum(values, -most), most).astype(kind)


def setup_inputs(seed: int = 0) -> dict:
    arg_keys = jax.random.split(jax.random.key(seed), 16)
    displacement = normal_values(arg_keys[0], (3, NODES), 1.0, 6.0, ((1, 32),), jnp.float32)
    disp_prev = normal_values(arg_keys[1], (3, NODES), 1.0, 6.0, ((1, 32),), jnp.float32)
    nodal_load = normal_values(arg_keys[2], (3, NODES), 1.0, 6.0, ((1, 32),), jnp.float32)
    nodal_mass = jnp.clip(jnp.exp(math.log(4.0) - 1.3862944 * jax.random.uniform(arg_keys[3], (NODES,), jnp.float32) ** levels(arg_keys[3], (NODES,), ((0, 32),), -0.2, 0.2)), 1.0, 4.0)
    modulus = jnp.clip(jnp.exp(math.log(10.0) - 2.3025851 * jax.random.uniform(arg_keys[4], (ELEMS,), jnp.float32) ** levels(arg_keys[4], (ELEMS,), ((0, 32),), -0.2, 0.2)), 1.0, 10.0)
    stiffness = draw_stiffness(jax.random.fold_in(arg_keys[15], 71), 0)
    connectivity = draw_connectivity(jax.random.fold_in(arg_keys[15], 71), 0)
    ghost_send = with_ends(jax.random.randint(arg_keys[7], (2, GHOSTS), 0, NODE_DEV), jax.random.fold_in(arg_keys[7], 1), 0, NODE_DEV - 1).astype(jnp.int32)
    contact_node = with_ends(jax.random.randint(arg_keys[8], (CONTACT,), 0, NODE_DEV), jax.random.fold_in(arg_keys[8], 1), 0, NODE_DEV - 1).astype(jnp.int32)
    contact_owner = draw_contact_owner(jax.random.fold_in(arg_keys[15], 71), 0)
    pair_ids = with_ends(jax.random.randint(arg_keys[10], (2, PAIRS), 0, 2 * CN_DEV), jax.random.fold_in(arg_keys[10], 1), 0, (2 * CN_DEV) - 1).astype(jnp.int32)
    gap_start = normal_values(arg_keys[11], (3, PAIRS), 0.5, 3.0, ((1, 32),), jnp.float32)
    penalty = jnp.clip(jnp.exp(math.log(2.0) - 1.3862944 * jax.random.uniform(arg_keys[12], (PAIRS,), jnp.float32) ** levels(arg_keys[12], (PAIRS,), ((0, 32),), -0.2, 0.2)), 0.5, 2.0)
    friction = jnp.clip(0.2 + 0.400000021 * jax.random.uniform(arg_keys[13], (PAIRS,), jnp.float32) ** levels(arg_keys[13], (PAIRS,), ((0, 32),), -0.2, 0.2), 0.2, 0.6)
    slip_state = with_ends((jax.random.randint(arg_keys[14], (STEPS, PAIRS), 0, 3) < 1).astype(jnp.int32), jax.random.fold_in(arg_keys[14], 1), 0, 1)
    return {"displacement": displacement, "disp_prev": disp_prev, "nodal_load": nodal_load, "nodal_mass": nodal_mass, "modulus": modulus, "stiffness": stiffness, "connectivity": connectivity, "ghost_send": ghost_send, "contact_node": contact_node, "contact_owner": contact_owner, "pair_ids": pair_ids, "gap_start": gap_start, "penalty": penalty, "friction": friction, "slip_state": slip_state}


time_step_sq = 0.05

def to_blocks(values, block_width):
    return values.reshape(values.shape[0], OWNER_TOTAL, block_width).transpose(1, 0, 2)

def from_blocks(values):
    return values.transpose(1, 0, 2).reshape(values.shape[1], -1)

def slot_rank(owners):
    onehot = (owners[:, None] == jnp.arange(OWNER_TOTAL, dtype=jnp.int32)[None, :]).astype(jnp.int32)
    earlier = jnp.cumsum(onehot, axis=0) - onehot
    return lax.optimization_barrier(jnp.sum(earlier * onehot, axis=1)).astype(jnp.int32)

def element_forces(extended, node_links, moduli, stiffness):
    gathered = extended[:, node_links].reshape(ELDOF, node_links.shape[1])
    product = jnp.dot(stiffness, gathered, precision=lax.Precision.HIGHEST) * moduli[None, :]
    return jnp.zeros_like(extended).at[:, node_links].add(product.reshape(3, ELNODE, node_links.shape[1]))

def contact_pair_forces(received_values, pair_ids, gap_start, penalty, friction, slipping):
    near_side = received_values[:, pair_ids[0]]
    far_side = received_values[:, pair_ids[1]]
    gap_vec = gap_start + far_side - near_side
    normal = penalty * jnp.maximum(-gap_vec[2], 0.0)
    tangent_gap = gap_vec[0:2]
    sticking = -0.5 * penalty[None, :] * tangent_gap
    length = jnp.sqrt(lax.optimization_barrier(jnp.sum(tangent_gap * tangent_gap, axis=0)) + 0.01)
    sliding = -friction[None, :] * normal[None, :] * tangent_gap / length[None, :]
    tangent = jnp.where(slipping[None, :] == 1, sliding, sticking)
    pair_force = jnp.concatenate([tangent, normal[None, :]], axis=0)
    result = jnp.zeros_like(received_values).at[:, pair_ids[1]].add(pair_force)
    return result.at[:, pair_ids[0]].add(-pair_force)

def lend_nodes(field_now, lend_ids):
    return field_now[:, lend_ids]

def add_ghosts(own_part, lend_ids, from_lower, from_upper):
    return own_part.at[:, lend_ids[0]].add(from_lower).at[:, lend_ids[1]].add(from_upper)

def fill_outbox(field_now, nodes, places):
    return jnp.zeros((3, OWNER_TOTAL * CAP), jnp.float32).at[:, places].set(field_now[:, nodes])

def take_back(returned, nodes, places):
    return jnp.zeros((3, NODE_DEV), jnp.float32).at[:, nodes].add(returned[:, places])

def one_device_forces(device_item, stiffness):
    return element_forces(device_item[0], device_item[1], device_item[2], stiffness)

def swap_owner(values):
    return values.reshape(OWNER_TOTAL, 3, OWNER_TOTAL, CAP).transpose(2, 1, 0, 3).reshape(OWNER_TOTAL, 3, OWNER_TOTAL * CAP)

def reference(displacement, disp_prev, nodal_load, nodal_mass, modulus, stiffness, connectivity, ghost_send, contact_node, contact_owner, pair_ids, gap_start, penalty, friction, slip_state):
    current = to_blocks(displacement, NODE_DEV)
    previous = to_blocks(disp_prev, NODE_DEV)
    loads = to_blocks(nodal_load, NODE_DEV)
    masses = nodal_mass.reshape(OWNER_TOTAL, 1, NODE_DEV)
    node_links = connectivity.reshape(ELNODE, OWNER_TOTAL, NE_DEV).transpose(1, 0, 2)
    moduli = modulus.reshape(OWNER_TOTAL, NE_DEV)
    lend_lists = ghost_send.reshape(2, OWNER_TOTAL, HB).transpose(1, 0, 2)
    contact_nodes = contact_node.reshape(OWNER_TOTAL, CN_DEV)
    contact_owners = contact_owner.reshape(OWNER_TOTAL, CN_DEV)
    places = contact_owners * CAP + jax.vmap(slot_rank)(contact_owners)
    contact_pair_lists = pair_ids.reshape(2, OWNER_TOTAL, PAIRS_PER_OWNER).transpose(1, 0, 2)
    gap_block_parts = to_blocks(gap_start, PAIRS_PER_OWNER)
    penalty_stiffnesses = penalty.reshape(OWNER_TOTAL, PAIRS_PER_OWNER)
    friction_coefficients = friction.reshape(OWNER_TOTAL, PAIRS_PER_OWNER)
    slip_flags = slip_state.reshape(STEPS, OWNER_TOTAL, PAIRS_PER_OWNER)
    blank_rim = jnp.zeros((1, 3, HB), jnp.float32)
    acceleration = current
    for tally_count in range(STEPS):
        outgoing = jax.vmap(lend_nodes)(current, lend_lists)
        lower_ghosts = jnp.concatenate([blank_rim, outgoing[:-1, :, 1]], axis=0)
        upper_ghosts = jnp.concatenate([outgoing[1:, :, 0], blank_rim], axis=0)
        extended = jnp.concatenate([current, lower_ghosts, upper_ghosts], axis=2)
        forces = lax.map(partial_forces(stiffness), (extended, node_links, moduli))
        from_upper = jnp.concatenate([forces[1:, :, NODE_DEV:NODE_DEV + HB], blank_rim], axis=0)
        from_lower = jnp.concatenate([blank_rim, forces[:-1, :, NODE_DEV + HB:]], axis=0)
        internal = jax.vmap(add_ghosts)(forces[:, :, :NODE_DEV], lend_lists, from_lower, from_upper)
        outboxes = jax.vmap(fill_outbox)(current, contact_nodes, places)
        received_values = swap_owner(outboxes)
        reply_messages = jax.vmap(contact_pair_forces)(received_values, contact_pair_lists, gap_block_parts, penalty_stiffnesses, friction_coefficients, slip_flags[tally_count])
        returned = swap_owner(reply_messages)
        contact = jax.vmap(take_back)(returned, contact_nodes, places)
        acceleration = (loads - internal + contact) / masses
        later = 2.0 * current - previous + time_step_sq * acceleration
        previous = current
        current = later
    return (from_blocks(current), from_blocks(acceleration))

def partial_forces(stiffness):

    def apply_one(device_item):
        return one_device_forces(device_item, stiffness)
    return apply_one
```

```python
import functools

import jax
import jax.numpy as jnp
from jax import lax
from jax.experimental import pallas as pl
from jax.experimental.pallas import tpu as pltpu
from jax.sharding import PartitionSpec as P

STEPS = 3
LANES = 128
SUBLANES = 8
MESH = pl.DeviceIdType.MESH

time_step_sq = 0.05


def matches(index_row, rows):
    return lax.broadcasted_iota(jnp.int32, (rows, index_row.shape[1]), 0) == index_row


def split(value):
    high = value.astype(jnp.bfloat16)
    return high, (value - high.astype(jnp.float32)).astype(jnp.bfloat16)


def side_by_side(table):
    return jnp.concatenate(split(table), axis=1)


def gather(table, lane_hot, row_index, rows):
    got = jnp.dot(
        table,
        jnp.concatenate([lane_hot, lane_hot], axis=0),
        preferred_element_type=jnp.float32,
    )
    mask = matches(row_index, rows)
    return [
        jnp.sum(jnp.where(mask, got[c * rows : (c + 1) * rows], 0.0), axis=0, keepdims=True)
        for c in range(3)
    ]


def scatter(values, lane_hot, row_index, rows):
    mask = matches(row_index, rows)
    parts = [split(value) for value in values]
    left = jnp.concatenate(
        [jnp.where(mask, parts[c][s].astype(jnp.float32), 0.0) for s in range(2) for c in range(3)],
        axis=0,
    ).astype(jnp.bfloat16)
    return lax.dot_general(
        left, lane_hot, (((1,), (1,)), ((), ())), preferred_element_type=jnp.float32
    )


def kernel(
    dims,
    idx,
    owner,
    node,
    mod,
    stiff,
    gap0,
    pen,
    fric,
    slip,
    disp,
    prev,
    load,
    mass,
    out_u,
    out_a,
    row_of,
    lane_hot,
    own_tab,
    ext,
    ext_tab,
    ue,
    fe,
    acc_e,
    acc_c,
    slot_vals,
    pair_vals,
    recv_tab,
    cur,
    old,
    box_out,
    box_in,
    halo_out,
    halo_in,
    box_send,
    box_recv,
    halo_send,
    halo_recv,
):
    n_py, n, cap, elnode, lent, width = dims
    px, py = lax.axis_index("px"), lax.axis_index("py")
    me = px * n_py + py

    def place(device):
        return {"px": lax.div(device, n_py), "py": lax.rem(device, n_py)}

    barrier = pltpu.get_barrier_semaphore()

    @pl.loop(1, n)
    def _(d):
        pl.semaphore_signal(
            barrier, inc=1, device_id=place(lax.rem(me + d, n)), device_id_type=MESH
        )

    own_rows = cur.shape[0] // 3
    ext_rows = ext.shape[0] // 3
    slots = slot_vals.shape[1]
    slot_rows = recv_tab.shape[0] // 3
    given = idx.shape[0]
    lend = elnode
    pair_chunks = pen.shape[1] // width
    near, far = elnode + 1, elnode + 1 + pair_chunks

    def set_row(k, row):
        row_of[pl.ds(k, 1), :] = lax.shift_right_arithmetic(row, 7)
        lane_hot[k] = jnp.where(matches(row & (LANES - 1), LANES), 1.0, 0.0).astype(jnp.bfloat16)

    @pl.loop(0, given)
    def _(k):
        set_row(k, idx[pl.ds(k, 1), :])

    before = (
        lax.broadcasted_iota(jnp.int32, (width, width), 0)
        < lax.broadcasted_iota(jnp.int32, (width, width), 1)
    )
    before = jnp.where(before, 1.0, 0.0).astype(jnp.bfloat16)
    carry = jnp.zeros((n, 1), jnp.float32)
    found = jnp.zeros((2 * slots, width), jnp.float32)
    for j in range(owner.shape[0]):
        target = owner[j : j + 1, :]
        mask = matches(target, n)
        hot = jnp.where(mask, 1.0, 0.0)
        earlier = jnp.dot(hot.astype(jnp.bfloat16), before, preferred_element_type=jnp.float32)
        rank = jnp.sum(jnp.where(mask, earlier + carry, 0.0), axis=0, keepdims=True)
        carry = carry + jnp.sum(hot, axis=1, keepdims=True)
        slot = target * cap + rank.astype(jnp.int32)
        mask = matches(lax.div(slot, width), slots)
        number = node[j : j + 1, :] + 1
        left = jnp.concatenate(
            [
                jnp.where(mask, lax.shift_right_arithmetic(number, 6).astype(jnp.float32), 0.0),
                jnp.where(mask, (number & 63).astype(jnp.float32), 0.0),
            ],
            axis=0,
        ).astype(jnp.bfloat16)
        right = jnp.where(matches(lax.rem(slot, width), width), 1.0, 0.0).astype(jnp.bfloat16)
        found = found + lax.dot_general(
            left, right, (((1,), (1,)), ((), ())), preferred_element_type=jnp.float32
        )
    numbers = (found[:slots] * 64.0 + found[slots:]).astype(jnp.int32) - 1
    for q in range(slots):
        set_row(given + q, numbers[q : q + 1, :])

    cur[...] = disp[...]
    old[...] = prev[...]
    ext[...] = jnp.zeros_like(ext)

    def box_copy(i, d):
        other = lax.rem(me + d, n)
        return pltpu.make_async_remote_copy(
            src_ref=box_out.at[i, other],
            dst_ref=box_in.at[i, me],
            send_sem=box_send.at[i],
            recv_sem=box_recv.at[i],
            device_id=place(other),
            device_id_type=MESH,
        )

    def box_start(i):
        @pl.loop(1, n)
        def _(d):
            box_copy(i, d).start()

        box_in[i, me] = box_out[i, me]

    def box_wait(i):
        every = pl.ds(0, n - 1)
        whole = pltpu.make_async_remote_copy(
            src_ref=box_out.at[i, every],
            dst_ref=box_in.at[i, every],
            send_sem=box_send.at[i],
            recv_sem=box_recv.at[i],
            device_id=place(lax.rem(me + 1, n)),
            device_id_type=MESH,
        )
        whole.wait()

    def halo_copies(i):
        copies = []
        for side, step in ((0, n - 1), (1, 1)):
            copies.append(
                pltpu.make_async_remote_copy(
                    src_ref=halo_out.at[i, side],
                    dst_ref=halo_in.at[i, 1 - side],
                    send_sem=halo_send.at[i, side],
                    recv_sem=halo_recv.at[i, 1 - side],
                    device_id=place(lax.rem(me + step, n)),
                    device_id_type=MESH,
                )
            )
        return copies

    def halo_start(i):
        for copy in halo_copies(i):
            copy.start()

    def halo_wait(i):
        for copy in halo_copies(i):
            copy.wait()

    def halo_side(i, side, c):
        inside = me > 0 if side == 0 else me < n - 1
        return jnp.where(inside, halo_in[i, side, c : c + 1, :], 0.0)

    lent_rows = lent // LANES

    for step in range(STEPS):
        going, back = 2 * step, 2 * step + 1
        own_tab[...] = side_by_side(cur[...])
        lending = gather(own_tab[...], lane_hot[lend], row_of[lend : lend + 1, :], own_rows)
        for c in range(3):
            for side in range(2):
                halo_out[going, side, c : c + 1, :] = lending[c][:, side * lent : (side + 1) * lent]
        if step == 0:
            pl.semaphore_wait(barrier, n - 1)
        halo_start(going)

        @pl.loop(0, slots)
        def _(q):
            k = given + q
            got = gather(own_tab[...], lane_hot[k], row_of[pl.ds(k, 1), :], own_rows)
            for c in range(3):
                slot_vals[c, pl.ds(q, 1), :] = got[c]

        for o in range(n):
            r, l = divmod(o * cap, width)
            for c in range(3):
                box_out[going, o, c : c + 1, :] = slot_vals[c, r : r + 1, l : l + cap]
        box_start(going)

        halo_wait(going)
        for c in range(3):
            ext[c * ext_rows : c * ext_rows + own_rows, :] = cur[c * own_rows : (c + 1) * own_rows, :]
            for side in range(2):
                ghosts = halo_side(going, side, c)
                for r in range(lent_rows):
                    at = c * ext_rows + own_rows + side * lent_rows + r
                    ext[at : at + 1, :] = ghosts[:, r * LANES : (r + 1) * LANES]
        ext_tab[...] = side_by_side(ext[...])

        @pl.loop(0, elnode)
        def _(k):
            got = gather(ext_tab[...], lane_hot[k], row_of[pl.ds(k, 1), :], ext_rows)
            for c in range(3):
                ue[pl.ds(c * elnode + k, 1), :] = got[c]

        box_wait(going)
        for g in range(n):
            r, l = divmod(g * cap, LANES)
            for c in range(3):
                at = c * slot_rows + r
                recv_tab[at : at + 1, l : l + cap] = box_in[going, g, c : c + 1, :]
        table = side_by_side(recv_tab[...])
        total = jnp.zeros((6 * slot_rows, LANES), jnp.float32)
        for p in range(pair_chunks):
            cols = slice(p * width, (p + 1) * width)
            near_rows, far_rows = row_of[near + p : near + p + 1, :], row_of[far + p : far + p + 1, :]
            low = gather(table, lane_hot[near + p], near_rows, slot_rows)
            high = gather(table, lane_hot[far + p], far_rows, slot_rows)
            gap = [gap0[c : c + 1, cols] + high[c] - low[c] for c in range(3)]
            normal = pen[:, cols] * jnp.maximum(-gap[2], 0.0)
            length = jnp.sqrt(gap[0] * gap[0] + gap[1] * gap[1] + 0.01)
            slipping = slip[step : step + 1, cols] == 1
            factor = jnp.where(
                slipping, -fric[:, cols] * normal / length, -0.5 * pen[:, cols]
            )
            force = [factor * gap[0], factor * gap[1], normal]
            total = total + scatter(force, lane_hot[far + p], far_rows, slot_rows)
            total = total - scatter(force, lane_hot[near + p], near_rows, slot_rows)
        pair_vals[...] = total[: 3 * slot_rows] + total[3 * slot_rows :]
        for g in range(n):
            r, l = divmod(g * cap, LANES)
            for c in range(3):
                at = c * slot_rows + r
                box_out[back, g, c : c + 1, :] = pair_vals[at : at + 1, l : l + cap]
        box_start(back)

        fe[...] = (
            jnp.dot(
                stiff[...],
                ue[...],
                precision=lax.Precision.HIGHEST,
                preferred_element_type=jnp.float32,
            )
            * mod[...]
        )
        acc_e[...] = jnp.zeros_like(acc_e)

        @pl.loop(0, elnode)
        def _(k):
            values = [fe[pl.ds(c * elnode + k, 1), :] for c in range(3)]
            acc_e[...] += scatter(values, lane_hot[k], row_of[pl.ds(k, 1), :], ext_rows)

        ext[...] = acc_e[: 3 * ext_rows] + acc_e[3 * ext_rows :]
        for c in range(3):
            for side in range(2):
                for r in range(lent_rows):
                    at = c * ext_rows + own_rows + side * lent_rows + r
                    halo_out[back, side, c : c + 1, r * LANES : (r + 1) * LANES] = ext[at : at + 1, :]
        halo_start(back)

        box_wait(back)
        for o in range(n):
            r, l = divmod(o * cap, width)
            for c in range(3):
                slot_vals[c, r : r + 1, l : l + cap] = box_in[back, o, c : c + 1, :]
        acc_c[...] = jnp.zeros_like(acc_c)

        @pl.loop(0, slots)
        def _(q):
            k = given + q
            values = [slot_vals[c, pl.ds(q, 1), :] for c in range(3)]
            acc_c[...] += scatter(values, lane_hot[k], row_of[pl.ds(k, 1), :], own_rows)

        halo_wait(back)
        values = [
            jnp.concatenate([halo_side(back, 0, c), halo_side(back, 1, c)], axis=1) for c in range(3)
        ]
        ghost = scatter(values, lane_hot[lend], row_of[lend : lend + 1, :], own_rows)
        total = acc_c[...] - ghost
        total = total[: 3 * own_rows] + total[3 * own_rows :]
        for c in range(3):
            rows = slice(c * own_rows, (c + 1) * own_rows)
            internal = ext[c * ext_rows : c * ext_rows + own_rows, :]
            acceleration = (load[rows, :] - internal + total[rows]) / mass[...]
            now = cur[rows, :]
            later = 2.0 * now - old[rows, :] + time_step_sq * acceleration
            old[rows, :] = now
            cur[rows, :] = later
            if step == STEPS - 1:
                out_u[rows, :] = later
                out_a[rows, :] = acceleration


def on_device(
    n_py,
    displacement,
    disp_prev,
    nodal_load,
    nodal_mass,
    modulus,
    stiffness,
    connectivity,
    ghost_send,
    contact_node,
    contact_owner,
    pair_ids,
    gap_start,
    penalty,
    friction,
    slip_state,
):
    n = lax.axis_size(("px", "py"))
    cap = 2 * contact_node.shape[0] // n
    elnode, width = connectivity.shape
    nodes = displacement.shape[1]
    lent = ghost_send.shape[1]
    own_rows = nodes // LANES
    ext_rows = -(-(own_rows + 2 * lent // LANES) // SUBLANES) * SUBLANES
    slots = n * cap // width
    slot_rows = n * cap // LANES
    idx = jnp.concatenate(
        [connectivity, ghost_send.reshape(1, 2 * lent), pair_ids.reshape(-1, width)], axis=0
    )
    chunks = idx.shape[0] + slots
    flat = (3 * own_rows, LANES)
    vmem = pl.BlockSpec(memory_space=pltpu.VMEM)
    f32, bf16 = jnp.float32, jnp.bfloat16
    dma = pltpu.SemaphoreType.DMA
    new_u, acc = pl.pallas_call(
        functools.partial(kernel, (n_py, n, cap, elnode, lent, width)),
        out_shape=[jax.ShapeDtypeStruct(flat, f32)] * 2,
        in_specs=[vmem] * 13,
        out_specs=[vmem] * 2,
        scratch_shapes=[
            pltpu.VMEM((chunks, width), jnp.int32),
            pltpu.VMEM((chunks, LANES, width), bf16),
            pltpu.VMEM((3 * own_rows, 2 * LANES), bf16),
            pltpu.VMEM((3 * ext_rows, LANES), f32),
            pltpu.VMEM((3 * ext_rows, 2 * LANES), bf16),
            pltpu.VMEM((3 * elnode, width), f32),
            pltpu.VMEM((3 * elnode, width), f32),
            pltpu.VMEM((6 * ext_rows, LANES), f32),
            pltpu.VMEM((6 * own_rows, LANES), f32),
            pltpu.VMEM((3, slots, width), f32),
            pltpu.VMEM((3 * slot_rows, LANES), f32),
            pltpu.VMEM((3 * slot_rows, LANES), f32),
            pltpu.VMEM(flat, f32),
            pltpu.VMEM(flat, f32),
            pltpu.VMEM((2 * STEPS, n, 3, cap), f32),
            pltpu.VMEM((2 * STEPS, n, 3, cap), f32),
            pltpu.VMEM((2 * STEPS, 2, 3, lent), f32),
            pltpu.VMEM((2 * STEPS, 2, 3, lent), f32),
            dma((2 * STEPS,)),
            dma((2 * STEPS,)),
            dma((2 * STEPS, 2)),
            dma((2 * STEPS, 2)),
        ],
        compiler_params=pltpu.CompilerParams(
            collective_id=0, has_side_effects=True, vmem_limit_bytes=48 * 1024 * 1024
        ),
        name="contact_steps",
    )(
        idx,
        contact_owner.reshape(-1, width),
        contact_node.reshape(-1, width),
        modulus.reshape(1, -1),
        stiffness,
        gap_start,
        penalty.reshape(1, -1),
        friction.reshape(1, -1),
        slip_state,
        displacement.reshape(flat),
        disp_prev.reshape(flat),
        nodal_load.reshape(flat),
        nodal_mass.reshape(-1, LANES),
    )
    return new_u.reshape(displacement.shape), acc.reshape(displacement.shape)


def solution(mesh):
    both = ("px", "py")
    row, cols = P(both), P(None, both)
    return jax.shard_map(
        functools.partial(on_device, mesh.shape["py"]),
        mesh=mesh,
        in_specs=(cols, cols, cols, row, row, P(), cols, cols, row, row, cols, cols, row, row, cols),
        out_specs=(cols, cols),
        check_vma=False,
    )
```

```python
import functools

import jax
import jax.numpy as jnp
from jax import lax
from jax.experimental import pallas as pl
from jax.experimental.pallas import tpu as pltpu
from jax.sharding import PartitionSpec as P

STEPS = 3
LANES = 128
SUBLANES = 8
MESH = pl.DeviceIdType.MESH

time_step_sq = 0.05


def matches(index_row, rows):
    return lax.broadcasted_iota(jnp.int32, (rows, index_row.shape[1]), 0) == index_row


def split(value):
    high = value.astype(jnp.bfloat16)
    return high, (value - high.astype(jnp.float32)).astype(jnp.bfloat16)


def gather(table, idx, start, rows):
    width = idx.shape[1]
    blocks = [idx[pl.ds(start, SUBLANES), l : l + LANES] for l in range(0, width, LANES)]
    row_of = [lax.shift_right_arithmetic(block, 7) for block in blocks]
    lane_of = [block & (LANES - 1) for block in blocks]
    got = [[jnp.zeros((SUBLANES, LANES), jnp.float32)] * len(blocks) for _ in range(3)]
    for r in range(rows):
        masks = [row == r for row in row_of]
        for c in range(3):
            at = c * rows + r
            line = jnp.broadcast_to(table[at : at + 1, :], (SUBLANES, LANES))
            for b, lane in enumerate(lane_of):
                value = jnp.take_along_axis(line, lane, axis=1, mode="promise_in_bounds")
                got[c][b] = jnp.where(masks[b], value, got[c][b])
    return [jnp.concatenate(parts, axis=1) for parts in got]


def scatter(values, lane_hot, row_index, rows):
    mask = matches(row_index, rows)
    parts = [split(value) for value in values]
    left = jnp.concatenate(
        [jnp.where(mask, parts[c][s].astype(jnp.float32), 0.0) for s in range(2) for c in range(3)],
        axis=0,
    ).astype(jnp.bfloat16)
    return lax.dot_general(
        left, lane_hot, (((1,), (1,)), ((), ())), preferred_element_type=jnp.float32
    )


def kernel(
    dims,
    given_idx,
    owner,
    node,
    mod,
    stiff,
    gap0,
    pen,
    fric,
    slip,
    disp,
    prev,
    load,
    mass,
    out_u,
    out_a,
    idx,
    lane_hot,
    stiff_wide,
    ext,
    ue,
    fe,
    acc_e,
    slot_vals,
    pair_vals,
    recv_tab,
    cur,
    old,
    box_out,
    box_in,
    halo_out,
    halo_in,
    box_send,
    box_recv,
    halo_send,
    halo_recv,
):
    n_py, n, cap, elnode, lent, width = dims
    px, py = lax.axis_index("px"), lax.axis_index("py")
    me = px * n_py + py

    def place(device):
        return {"px": lax.div(device, n_py), "py": lax.rem(device, n_py)}

    barrier = pltpu.get_barrier_semaphore()

    @pl.loop(1, n)
    def _(d):
        pl.semaphore_signal(
            barrier, inc=1, device_id=place(lax.rem(me + d, n)), device_id_type=MESH
        )

    own_rows = cur.shape[0] // 3
    ext_rows = ext.shape[0] // 3
    slots = slot_vals.shape[1]
    slot_rows = recv_tab.shape[0] // 3
    given = given_idx.shape[0]
    wide = stiff_wide.shape[0] // 3
    lend = wide
    pair_chunks = pen.shape[1] // width
    near, far = lend + 1, lend + 1 + pair_chunks

    def set_row(k, row):
        idx[pl.ds(k, 1), :] = row
        lane_hot[k] = jnp.where(matches(row & (LANES - 1), LANES), 1.0, 0.0).astype(jnp.bfloat16)

    def scatter_row(values, k, rows):
        row = lax.shift_right_arithmetic(idx[pl.ds(k, 1), :], 7)
        return scatter(values, lane_hot[k], row, rows)

    @pl.loop(0, given)
    def _(k):
        set_row(k, given_idx[pl.ds(k, 1), :])

    stiff_wide[...] = jnp.zeros_like(stiff_wide)
    for c in range(3):
        for d in range(3):
            stiff_wide[c * wide : c * wide + elnode, d * wide : d * wide + elnode] = stiff[
                c * elnode : (c + 1) * elnode, d * elnode : (d + 1) * elnode
            ]

    before = (
        lax.broadcasted_iota(jnp.int32, (width, width), 0)
        < lax.broadcasted_iota(jnp.int32, (width, width), 1)
    )
    before = jnp.where(before, 1.0, 0.0).astype(jnp.bfloat16)
    carry = jnp.zeros((n, 1), jnp.float32)
    found = jnp.zeros((2 * slots, width), jnp.float32)
    for j in range(owner.shape[0]):
        target = owner[j : j + 1, :]
        mask = matches(target, n)
        hot = jnp.where(mask, 1.0, 0.0)
        earlier = jnp.dot(hot.astype(jnp.bfloat16), before, preferred_element_type=jnp.float32)
        rank = jnp.sum(jnp.where(mask, earlier + carry, 0.0), axis=0, keepdims=True)
        carry = carry + jnp.sum(hot, axis=1, keepdims=True)
        slot = target * cap + rank.astype(jnp.int32)
        mask = matches(lax.div(slot, width), slots)
        number = node[j : j + 1, :] + 1
        left = jnp.concatenate(
            [
                jnp.where(mask, lax.shift_right_arithmetic(number, 6).astype(jnp.float32), 0.0),
                jnp.where(mask, (number & 63).astype(jnp.float32), 0.0),
            ],
            axis=0,
        ).astype(jnp.bfloat16)
        right = jnp.where(matches(lax.rem(slot, width), width), 1.0, 0.0).astype(jnp.bfloat16)
        found = found + lax.dot_general(
            left, right, (((1,), (1,)), ((), ())), preferred_element_type=jnp.float32
        )
    numbers = (found[:slots] * 64.0 + found[slots:]).astype(jnp.int32) - 1
    for q in range(slots):
        set_row(given + q, numbers[q : q + 1, :])

    cur[...] = disp[...]
    old[...] = prev[...]
    ext[...] = jnp.zeros_like(ext)

    def box_copy(i, d):
        other = lax.rem(me + d, n)
        return pltpu.make_async_remote_copy(
            src_ref=box_out.at[i, other],
            dst_ref=box_in.at[i, me],
            send_sem=box_send.at[i],
            recv_sem=box_recv.at[i],
            device_id=place(other),
            device_id_type=MESH,
        )

    def box_start(i):
        @pl.loop(1, n)
        def _(d):
            box_copy(i, d).start()

        box_in[i, me] = box_out[i, me]

    def box_wait(i):
        every = pl.ds(0, n - 1)
        whole = pltpu.make_async_remote_copy(
            src_ref=box_out.at[i, every],
            dst_ref=box_in.at[i, every],
            send_sem=box_send.at[i],
            recv_sem=box_recv.at[i],
            device_id=place(lax.rem(me + 1, n)),
            device_id_type=MESH,
        )
        whole.wait()

    def halo_copies(i):
        copies = []
        for side, step in ((0, n - 1), (1, 1)):
            copies.append(
                pltpu.make_async_remote_copy(
                    src_ref=halo_out.at[i, side],
                    dst_ref=halo_in.at[i, 1 - side],
                    send_sem=halo_send.at[i, side],
                    recv_sem=halo_recv.at[i, 1 - side],
                    device_id=place(lax.rem(me + step, n)),
                    device_id_type=MESH,
                )
            )
        return copies

    def halo_start(i):
        for copy in halo_copies(i):
            copy.start()

    def halo_wait(i):
        for copy in halo_copies(i):
            copy.wait()

    def halo_side(i, side, c):
        inside = me > 0 if side == 0 else me < n - 1
        return jnp.where(inside, halo_in[i, side, c : c + 1, :], 0.0)

    lent_rows = lent // LANES

    for step in range(STEPS):
        going, back = 2 * step, 2 * step + 1
        lending = [value[:1] for value in gather(cur, idx, lend, own_rows)]
        for c in range(3):
            for side in range(2):
                halo_out[going, side, c : c + 1, :] = lending[c][:, side * lent : (side + 1) * lent]
        if step == 0:
            pl.semaphore_wait(barrier, n - 1)
        halo_start(going)

        for q in range(0, slots, SUBLANES):
            got = gather(cur, idx, given + q, own_rows)
            for c in range(3):
                slot_vals[c, q : q + SUBLANES, :] = got[c]

        for o in range(n):
            r, l = divmod(o * cap, width)
            for c in range(3):
                box_out[going, o, c : c + 1, :] = slot_vals[c, r : r + 1, l : l + cap]
        box_start(going)

        halo_wait(going)
        for c in range(3):
            ext[c * ext_rows : c * ext_rows + own_rows, :] = cur[c * own_rows : (c + 1) * own_rows, :]
            for side in range(2):
                ghosts = halo_side(going, side, c)
                for r in range(lent_rows):
                    at = c * ext_rows + own_rows + side * lent_rows + r
                    ext[at : at + 1, :] = ghosts[:, r * LANES : (r + 1) * LANES]

        @pl.loop(0, wide // SUBLANES)
        def _(group):
            start = pl.multiple_of(group * SUBLANES, SUBLANES)
            got = gather(ext, idx, start, ext_rows)
            for c in range(3):
                ue[pl.ds(pl.multiple_of(c * wide + start, SUBLANES), SUBLANES), :] = got[c]

        box_wait(going)
        for g in range(n):
            r, l = divmod(g * cap, LANES)
            for c in range(3):
                at = c * slot_rows + r
                recv_tab[at : at + 1, l : l + cap] = box_in[going, g, c : c + 1, :]
        ends = gather(recv_tab, idx, lend, slot_rows)
        total = jnp.zeros((6 * slot_rows, LANES), jnp.float32)
        for p in range(pair_chunks):
            cols = slice(p * width, (p + 1) * width)
            low = [value[1 + p : 2 + p] for value in ends]
            high = [value[1 + pair_chunks + p : 2 + pair_chunks + p] for value in ends]
            gap = [gap0[c : c + 1, cols] + high[c] - low[c] for c in range(3)]
            normal = pen[:, cols] * jnp.maximum(-gap[2], 0.0)
            length = jnp.sqrt(gap[0] * gap[0] + gap[1] * gap[1] + 0.01)
            slipping = slip[step : step + 1, cols] == 1
            factor = jnp.where(
                slipping, -fric[:, cols] * normal / length, -0.5 * pen[:, cols]
            )
            force = [factor * gap[0], factor * gap[1], normal]
            total = total + scatter_row(force, far + p, slot_rows)
            total = total - scatter_row(force, near + p, slot_rows)
        pair_vals[...] = total[: 3 * slot_rows] + total[3 * slot_rows :]
        for g in range(n):
            r, l = divmod(g * cap, LANES)
            for c in range(3):
                at = c * slot_rows + r
                box_out[back, g, c : c + 1, :] = pair_vals[at : at + 1, l : l + cap]
        box_start(back)

        fe[...] = (
            jnp.dot(
                stiff_wide[...],
                ue[...],
                precision=lax.Precision.HIGHEST,
                preferred_element_type=jnp.float32,
            )
            * mod[...]
        )
        acc_e[...] = jnp.zeros_like(acc_e)

        some = next(f for f in (9, 3, 1) if elnode % f == 0)

        @pl.loop(0, elnode // some)
        def _(group):
            total = acc_e[...]
            for i in range(some):
                k = group * some + i
                values = [fe[pl.ds(c * wide + k, 1), :] for c in range(3)]
                total = total + scatter_row(values, k, ext_rows)
            acc_e[...] = total

        ext[...] = acc_e[: 3 * ext_rows] + acc_e[3 * ext_rows :]
        for c in range(3):
            for side in range(2):
                for r in range(lent_rows):
                    at = c * ext_rows + own_rows + side * lent_rows + r
                    halo_out[back, side, c : c + 1, r * LANES : (r + 1) * LANES] = ext[at : at + 1, :]
        halo_start(back)

        box_wait(back)
        for o in range(n):
            r, l = divmod(o * cap, width)
            for c in range(3):
                slot_vals[c, r : r + 1, l : l + cap] = box_in[back, o, c : c + 1, :]
        contact = jnp.zeros((6 * own_rows, LANES), jnp.float32)
        for q in range(slots):
            values = [slot_vals[c, q : q + 1, :] for c in range(3)]
            contact = contact + scatter_row(values, given + q, own_rows)

        halo_wait(back)
        values = [
            jnp.concatenate([halo_side(back, 0, c), halo_side(back, 1, c)], axis=1) for c in range(3)
        ]
        total = contact - scatter_row(values, lend, own_rows)
        total = total[: 3 * own_rows] + total[3 * own_rows :]
        for c in range(3):
            rows = slice(c * own_rows, (c + 1) * own_rows)
            internal = ext[c * ext_rows : c * ext_rows + own_rows, :]
            acceleration = (load[rows, :] - internal + total[rows]) / mass[...]
            now = cur[rows, :]
            later = 2.0 * now - old[rows, :] + time_step_sq * acceleration
            old[rows, :] = now
            cur[rows, :] = later
            if step == STEPS - 1:
                out_u[rows, :] = later
                out_a[rows, :] = acceleration


def on_device(
    n_py,
    displacement,
    disp_prev,
    nodal_load,
    nodal_mass,
    modulus,
    stiffness,
    connectivity,
    ghost_send,
    contact_node,
    contact_owner,
    pair_ids,
    gap_start,
    penalty,
    friction,
    slip_state,
):
    n = lax.axis_size(("px", "py"))
    cap = 2 * contact_node.shape[0] // n
    elnode, width = connectivity.shape
    nodes = displacement.shape[1]
    lent = ghost_send.shape[1]
    own_rows = nodes // LANES
    ext_rows = -(-(own_rows + 2 * lent // LANES) // SUBLANES) * SUBLANES
    slots = n * cap // width
    slot_rows = n * cap // LANES
    wide = -(-elnode // SUBLANES) * SUBLANES
    pairs = pair_ids.reshape(-1, width)
    idx = jnp.concatenate(
        [
            jnp.pad(connectivity, ((0, wide - elnode), (0, 0)), constant_values=-1),
            ghost_send.reshape(1, 2 * lent),
            jnp.pad(pairs, ((0, -(1 + pairs.shape[0]) % SUBLANES), (0, 0)), constant_values=-1),
        ],
        axis=0,
    )
    chunks = idx.shape[0] + slots
    flat = (3 * own_rows, LANES)
    vmem = pl.BlockSpec(memory_space=pltpu.VMEM)
    f32, bf16 = jnp.float32, jnp.bfloat16
    dma = pltpu.SemaphoreType.DMA
    new_u, acc = pl.pallas_call(
        functools.partial(kernel, (n_py, n, cap, elnode, lent, width)),
        out_shape=[jax.ShapeDtypeStruct(flat, f32)] * 2,
        in_specs=[vmem] * 13,
        out_specs=[vmem] * 2,
        scratch_shapes=[
            pltpu.VMEM((chunks, width), jnp.int32),
            pltpu.VMEM((chunks, LANES, width), bf16),
            pltpu.VMEM((3 * wide, 3 * wide), f32),
            pltpu.VMEM((3 * ext_rows, LANES), f32),
            pltpu.VMEM((3 * wide, width), f32),
            pltpu.VMEM((3 * wide, width), f32),
            pltpu.VMEM((6 * ext_rows, LANES), f32),
            pltpu.VMEM((3, slots, width), f32),
            pltpu.VMEM((3 * slot_rows, LANES), f32),
            pltpu.VMEM((3 * slot_rows, LANES), f32),
            pltpu.VMEM(flat, f32),
            pltpu.VMEM(flat, f32),
            pltpu.VMEM((2 * STEPS, n, 3, cap), f32),
            pltpu.VMEM((2 * STEPS, n, 3, cap), f32),
            pltpu.VMEM((2 * STEPS, 2, 3, lent), f32),
            pltpu.VMEM((2 * STEPS, 2, 3, lent), f32),
            dma((2 * STEPS,)),
            dma((2 * STEPS,)),
            dma((2 * STEPS, 2)),
            dma((2 * STEPS, 2)),
        ],
        compiler_params=pltpu.CompilerParams(
            collective_id=0, has_side_effects=True, vmem_limit_bytes=48 * 1024 * 1024
        ),
        name="contact_steps",
    )(
        idx,
        contact_owner.reshape(-1, width),
        contact_node.reshape(-1, width),
        modulus.reshape(1, -1),
        stiffness,
        gap_start,
        penalty.reshape(1, -1),
        friction.reshape(1, -1),
        slip_state,
        displacement.reshape(flat),
        disp_prev.reshape(flat),
        nodal_load.reshape(flat),
        nodal_mass.reshape(-1, LANES),
    )
    return new_u.reshape(displacement.shape), acc.reshape(displacement.shape)


def solution(mesh):
    both = ("px", "py")
    row, cols = P(both), P(None, both)
    return jax.shard_map(
        functools.partial(on_device, mesh.shape["py"]),
        mesh=mesh,
        in_specs=(cols, cols, cols, row, row, P(), cols, cols, row, row, cols, cols, row, row, cols),
        out_specs=(cols, cols),
        check_vma=False,
    )
```

```python
import functools

import jax
import jax.numpy as jnp
from jax import lax
from jax.experimental import pallas as pl
from jax.experimental.pallas import tpu as pltpu
from jax.sharding import PartitionSpec as P

STEPS = 3
LANES = 128
SUBLANES = 8
MESH = pl.DeviceIdType.MESH

time_step_sq = 0.05


def matches(index_row, rows):
    return lax.broadcasted_iota(jnp.int32, (rows, index_row.shape[1]), 0) == index_row


def split(value):
    high = value.astype(jnp.bfloat16)
    return high, (value - high.astype(jnp.float32)).astype(jnp.bfloat16)


def gather_block(table, index, rows, used):
    row_of = lax.shift_right_arithmetic(index, 7)
    lane_of = index & (LANES - 1)
    got = [jnp.zeros((SUBLANES, LANES), jnp.float32)] * 3
    for r in range(used):
        mask = row_of == r
        for c in range(3):
            at = c * rows + r
            line = jnp.broadcast_to(table[at : at + 1, :], (SUBLANES, LANES))
            value = jnp.take_along_axis(line, lane_of, axis=1, mode="promise_in_bounds")
            got[c] = jnp.where(mask, value, got[c])
    return got


def scatter(values, lane_hot, row_index, rows):
    mask = matches(row_index, rows)
    parts = [split(value) for value in values]
    left = jnp.concatenate(
        [jnp.where(mask, parts[c][s].astype(jnp.float32), 0.0) for s in range(2) for c in range(3)],
        axis=0,
    ).astype(jnp.bfloat16)
    return lax.dot_general(
        left, lane_hot, (((1,), (1,)), ((), ())), preferred_element_type=jnp.float32
    )


def kernel(
    dims,
    given_idx,
    lend_idx,
    owner,
    node,
    mod,
    stiff,
    gap0,
    pen,
    fric,
    slip,
    disp,
    prev,
    load,
    mass,
    out_u,
    out_a,
    idx,
    lane_hot,
    stiff_wide,
    ext,
    ue,
    fe,
    acc_e,
    slot_vals,
    ends,
    pair_vals,
    recv_tab,
    cur,
    old,
    box_out,
    box_in,
    halo_out,
    halo_in,
    box_send,
    box_recv,
    halo_send,
    halo_recv,
):
    n_py, n, cap, elnode, lent, width = dims
    px, py = lax.axis_index("px"), lax.axis_index("py")
    me = px * n_py + py

    def place(device):
        return {"px": lax.div(device, n_py), "py": lax.rem(device, n_py)}

    barrier = pltpu.get_barrier_semaphore()

    @pl.loop(1, n)
    def _(d):
        pl.semaphore_signal(
            barrier, inc=1, device_id=place(lax.rem(me + d, n)), device_id_type=MESH
        )

    own_rows = cur.shape[0] // 3
    ext_rows = ext.shape[0] // 3
    slots = slot_vals.shape[1]
    slot_rows = recv_tab.shape[0] // 3
    given = given_idx.shape[0]
    wide = stiff_wide.shape[0] // 3
    lend = wide
    pair_chunks = pen.shape[1] // width
    near, far = lend + 1, lend + 1 + pair_chunks

    def set_row(k, row):
        idx[pl.ds(k, 1), :] = row
        lane_hot[k] = jnp.where(matches(row & (LANES - 1), LANES), 1.0, 0.0).astype(jnp.bfloat16)

    def scatter_row(values, k, rows):
        row = lax.shift_right_arithmetic(idx[pl.ds(k, 1), :], 7)
        return scatter(values, lane_hot[k], row, rows)

    @pl.loop(0, given)
    def _(k):
        set_row(k, given_idx[pl.ds(k, 1), :])

    stiff_wide[...] = jnp.zeros_like(stiff_wide)
    for c in range(3):
        for d in range(3):
            stiff_wide[c * wide : c * wide + elnode, d * wide : d * wide + elnode] = stiff[
                c * elnode : (c + 1) * elnode, d * elnode : (d + 1) * elnode
            ]

    before = (
        lax.broadcasted_iota(jnp.int32, (width, width), 0)
        < lax.broadcasted_iota(jnp.int32, (width, width), 1)
    )
    before = jnp.where(before, 1.0, 0.0).astype(jnp.bfloat16)
    carry = jnp.zeros((n, 1), jnp.float32)
    found = jnp.zeros((2 * slots, width), jnp.float32)
    for j in range(owner.shape[0]):
        target = owner[j : j + 1, :]
        mask = matches(target, n)
        hot = jnp.where(mask, 1.0, 0.0)
        earlier = jnp.dot(hot.astype(jnp.bfloat16), before, preferred_element_type=jnp.float32)
        rank = jnp.sum(jnp.where(mask, earlier + carry, 0.0), axis=0, keepdims=True)
        carry = carry + jnp.sum(hot, axis=1, keepdims=True)
        slot = target * cap + rank.astype(jnp.int32)
        mask = matches(lax.div(slot, width), slots)
        number = node[j : j + 1, :] + 1
        left = jnp.concatenate(
            [
                jnp.where(mask, lax.shift_right_arithmetic(number, 6).astype(jnp.float32), 0.0),
                jnp.where(mask, (number & 63).astype(jnp.float32), 0.0),
            ],
            axis=0,
        ).astype(jnp.bfloat16)
        right = jnp.where(matches(lax.rem(slot, width), width), 1.0, 0.0).astype(jnp.bfloat16)
        found = found + lax.dot_general(
            left, right, (((1,), (1,)), ((), ())), preferred_element_type=jnp.float32
        )
    numbers = (found[:slots] * 64.0 + found[slots:]).astype(jnp.int32) - 1
    for q in range(slots):
        set_row(given + q, numbers[q : q + 1, :])

    cur[...] = disp[...]
    old[...] = prev[...]
    ext[...] = jnp.zeros_like(ext)

    def box_copy(i, d):
        other = lax.rem(me + d, n)
        return pltpu.make_async_remote_copy(
            src_ref=box_out.at[i, other],
            dst_ref=box_in.at[i, me],
            send_sem=box_send.at[i],
            recv_sem=box_recv.at[i],
            device_id=place(other),
            device_id_type=MESH,
        )

    def box_start(i):
        @pl.loop(1, n)
        def _(d):
            box_copy(i, d).start()

        box_in[i, me] = box_out[i, me]

    def box_wait(i):
        every = pl.ds(0, n - 1)
        whole = pltpu.make_async_remote_copy(
            src_ref=box_out.at[i, every],
            dst_ref=box_in.at[i, every],
            send_sem=box_send.at[i],
            recv_sem=box_recv.at[i],
            device_id=place(lax.rem(me + 1, n)),
            device_id_type=MESH,
        )
        whole.wait()

    def halo_copies(i):
        copies = []
        for side, step in ((0, n - 1), (1, 1)):
            copies.append(
                pltpu.make_async_remote_copy(
                    src_ref=halo_out.at[i, side],
                    dst_ref=halo_in.at[i, 1 - side],
                    send_sem=halo_send.at[i, side],
                    recv_sem=halo_recv.at[i, 1 - side],
                    device_id=place(lax.rem(me + step, n)),
                    device_id_type=MESH,
                )
            )
        return copies

    def halo_start(i):
        for copy in halo_copies(i):
            copy.start()

    def halo_wait(i):
        for copy in halo_copies(i):
            copy.wait()

    def halo_side(i, side, c):
        inside = me > 0 if side == 0 else me < n - 1
        return jnp.where(inside, halo_in[i, side, c : c + 1, :], 0.0)

    lent_rows = lent // LANES
    blocks = width // LANES

    def gather_rows(table, first, count, rows, used, store):
        @pl.loop(0, count // SUBLANES * blocks, unroll=2)
        def _(i):
            row = pl.multiple_of(lax.div(i, blocks) * SUBLANES, SUBLANES)
            lane = pl.multiple_of(lax.rem(i, blocks) * LANES, LANES)
            index = idx[pl.ds(first + row, SUBLANES), pl.ds(lane, LANES)]
            for c, value in enumerate(gather_block(table, index, rows, used)):
                store(c, pl.ds(row, SUBLANES), pl.ds(lane, LANES), value)

    def slot_store(c, rows, lanes, value):
        slot_vals[c, rows, lanes] = value

    def element_store(c, rows, lanes, value):
        ue[c, rows, lanes] = value

    def end_store(c, rows, lanes, value):
        ends[c, rows, lanes] = value

    for step in range(STEPS):
        going, back = 2 * step, 2 * step + 1
        lending = gather_block(cur, lend_idx[...], own_rows, own_rows)
        for c in range(3):
            for side in range(2):
                for r in range(lent_rows):
                    at = side * lent_rows + r
                    halo_out[going, side, c : c + 1, r * LANES : (r + 1) * LANES] = lending[c][
                        at : at + 1
                    ]
        if step == 0:
            pl.semaphore_wait(barrier, n - 1)
        halo_start(going)

        gather_rows(cur, given, slots, own_rows, own_rows, slot_store)

        for o in range(n):
            r, l = divmod(o * cap, width)
            for c in range(3):
                box_out[going, o, c : c + 1, :] = slot_vals[c, r : r + 1, l : l + cap]
        box_start(going)

        halo_wait(going)
        for c in range(3):
            ext[c * ext_rows : c * ext_rows + own_rows, :] = cur[c * own_rows : (c + 1) * own_rows, :]
            for side in range(2):
                ghosts = halo_side(going, side, c)
                for r in range(lent_rows):
                    at = c * ext_rows + own_rows + side * lent_rows + r
                    ext[at : at + 1, :] = ghosts[:, r * LANES : (r + 1) * LANES]

        gather_rows(ext, 0, wide, ext_rows, own_rows + 2 * lent_rows, element_store)

        box_wait(going)
        for g in range(n):
            r, l = divmod(g * cap, LANES)
            for c in range(3):
                at = c * slot_rows + r
                recv_tab[at : at + 1, l : l + cap] = box_in[going, g, c : c + 1, :]
        gather_rows(recv_tab, lend, SUBLANES, slot_rows, slot_rows, end_store)
        total = jnp.zeros((6 * slot_rows, LANES), jnp.float32)
        for p in range(pair_chunks):
            cols = slice(p * width, (p + 1) * width)
            low = [ends[c, 1 + p : 2 + p, :] for c in range(3)]
            high = [ends[c, 1 + pair_chunks + p : 2 + pair_chunks + p, :] for c in range(3)]
            gap = [gap0[c : c + 1, cols] + high[c] - low[c] for c in range(3)]
            normal = pen[:, cols] * jnp.maximum(-gap[2], 0.0)
            length = jnp.sqrt(gap[0] * gap[0] + gap[1] * gap[1] + 0.01)
            slipping = slip[step : step + 1, cols] == 1
            factor = jnp.where(
                slipping, -fric[:, cols] * normal / length, -0.5 * pen[:, cols]
            )
            force = [factor * gap[0], factor * gap[1], normal]
            total = total + scatter_row(force, far + p, slot_rows)
            total = total - scatter_row(force, near + p, slot_rows)
        pair_vals[...] = total[: 3 * slot_rows] + total[3 * slot_rows :]
        for g in range(n):
            r, l = divmod(g * cap, LANES)
            for c in range(3):
                at = c * slot_rows + r
                box_out[back, g, c : c + 1, :] = pair_vals[at : at + 1, l : l + cap]
        box_start(back)

        fe[...] = (
            jnp.dot(
                stiff_wide[...],
                ue[...].reshape(3 * wide, width),
                precision=lax.Precision.HIGHEST,
                preferred_element_type=jnp.float32,
            )
            * mod[...]
        )
        acc_e[...] = jnp.zeros_like(acc_e)

        some = next(f for f in (9, 3, 1) if elnode % f == 0)

        @pl.loop(0, elnode // some)
        def _(group):
            total = acc_e[...]
            for i in range(some):
                k = group * some + i
                values = [fe[pl.ds(c * wide + k, 1), :] for c in range(3)]
                total = total + scatter_row(values, k, ext_rows)
            acc_e[...] = total

        ext[...] = acc_e[: 3 * ext_rows] + acc_e[3 * ext_rows :]
        for c in range(3):
            for side in range(2):
                for r in range(lent_rows):
                    at = c * ext_rows + own_rows + side * lent_rows + r
                    halo_out[back, side, c : c + 1, r * LANES : (r + 1) * LANES] = ext[at : at + 1, :]
        halo_start(back)

        box_wait(back)
        for o in range(n):
            r, l = divmod(o * cap, width)
            for c in range(3):
                slot_vals[c, r : r + 1, l : l + cap] = box_in[back, o, c : c + 1, :]
        contact = jnp.zeros((6 * own_rows, LANES), jnp.float32)
        for q in range(slots):
            values = [slot_vals[c, q : q + 1, :] for c in range(3)]
            contact = contact + scatter_row(values, given + q, own_rows)

        halo_wait(back)
        values = [
            jnp.concatenate([halo_side(back, 0, c), halo_side(back, 1, c)], axis=1) for c in range(3)
        ]
        total = contact - scatter_row(values, lend, own_rows)
        total = total[: 3 * own_rows] + total[3 * own_rows :]
        for c in range(3):
            rows = slice(c * own_rows, (c + 1) * own_rows)
            internal = ext[c * ext_rows : c * ext_rows + own_rows, :]
            acceleration = (load[rows, :] - internal + total[rows]) / mass[...]
            now = cur[rows, :]
            later = 2.0 * now - old[rows, :] + time_step_sq * acceleration
            old[rows, :] = now
            cur[rows, :] = later
            if step == STEPS - 1:
                out_u[rows, :] = later
                out_a[rows, :] = acceleration


def on_device(
    n_py,
    displacement,
    disp_prev,
    nodal_load,
    nodal_mass,
    modulus,
    stiffness,
    connectivity,
    ghost_send,
    contact_node,
    contact_owner,
    pair_ids,
    gap_start,
    penalty,
    friction,
    slip_state,
):
    n = lax.axis_size(("px", "py"))
    cap = 2 * contact_node.shape[0] // n
    elnode, width = connectivity.shape
    nodes = displacement.shape[1]
    lent = ghost_send.shape[1]
    own_rows = nodes // LANES
    ext_rows = -(-(own_rows + 2 * lent // LANES) // SUBLANES) * SUBLANES
    slots = n * cap // width
    slot_rows = n * cap // LANES
    wide = -(-elnode // SUBLANES) * SUBLANES
    pairs = pair_ids.reshape(-1, width)
    idx = jnp.concatenate(
        [
            jnp.pad(connectivity, ((0, wide - elnode), (0, 0)), constant_values=-1),
            ghost_send.reshape(1, 2 * lent),
            jnp.pad(pairs, ((0, -(1 + pairs.shape[0]) % SUBLANES), (0, 0)), constant_values=-1),
        ],
        axis=0,
    )
    lend_idx = ghost_send.reshape(-1, LANES)
    lend_idx = jnp.pad(lend_idx, ((0, -lend_idx.shape[0] % SUBLANES), (0, 0)), constant_values=-1)
    chunks = idx.shape[0] + slots
    flat = (3 * own_rows, LANES)
    vmem = pl.BlockSpec(memory_space=pltpu.VMEM)
    f32, bf16 = jnp.float32, jnp.bfloat16
    dma = pltpu.SemaphoreType.DMA
    new_u, acc = pl.pallas_call(
        functools.partial(kernel, (n_py, n, cap, elnode, lent, width)),
        out_shape=[jax.ShapeDtypeStruct(flat, f32)] * 2,
        in_specs=[vmem] * 14,
        out_specs=[vmem] * 2,
        scratch_shapes=[
            pltpu.VMEM((chunks, width), jnp.int32),
            pltpu.VMEM((chunks, LANES, width), bf16),
            pltpu.VMEM((3 * wide, 3 * wide), f32),
            pltpu.VMEM((3 * ext_rows, LANES), f32),
            pltpu.VMEM((3, wide, width), f32),
            pltpu.VMEM((3 * wide, width), f32),
            pltpu.VMEM((6 * ext_rows, LANES), f32),
            pltpu.VMEM((3, slots, width), f32),
            pltpu.VMEM((3, SUBLANES, width), f32),
            pltpu.VMEM((3 * slot_rows, LANES), f32),
            pltpu.VMEM((3 * slot_rows, LANES), f32),
            pltpu.VMEM(flat, f32),
            pltpu.VMEM(flat, f32),
            pltpu.VMEM((2 * STEPS, n, 3, cap), f32),
            pltpu.VMEM((2 * STEPS, n, 3, cap), f32),
            pltpu.VMEM((2 * STEPS, 2, 3, lent), f32),
            pltpu.VMEM((2 * STEPS, 2, 3, lent), f32),
            dma((2 * STEPS,)),
            dma((2 * STEPS,)),
            dma((2 * STEPS, 2)),
            dma((2 * STEPS, 2)),
        ],
        compiler_params=pltpu.CompilerParams(
            collective_id=0, has_side_effects=True, vmem_limit_bytes=48 * 1024 * 1024
        ),
        name="contact_steps",
    )(
        idx,
        lend_idx,
        contact_owner.reshape(-1, width),
        contact_node.reshape(-1, width),
        modulus.reshape(1, -1),
        stiffness,
        gap_start,
        penalty.reshape(1, -1),
        friction.reshape(1, -1),
        slip_state,
        displacement.reshape(flat),
        disp_prev.reshape(flat),
        nodal_load.reshape(flat),
        nodal_mass.reshape(-1, LANES),
    )
    return new_u.reshape(displacement.shape), acc.reshape(displacement.shape)


def solution(mesh):
    both = ("px", "py")
    row, cols = P(both), P(None, both)
    return jax.shard_map(
        functools.partial(on_device, mesh.shape["py"]),
        mesh=mesh,
        in_specs=(cols, cols, cols, row, row, P(), cols, cols, row, row, cols, cols, row, row, cols),
        out_specs=(cols, cols),
        check_vma=False,
    )
```

```python
import functools

import jax
import jax.numpy as jnp
from jax import lax
from jax.experimental import pallas as pl
from jax.experimental.pallas import tpu as pltpu
from jax.sharding import PartitionSpec as P

STEPS = 3
LANES = 128
SUBLANES = 8
MESH = pl.DeviceIdType.MESH

time_step_sq = 0.05


def matches(index_row, rows):
    return lax.broadcasted_iota(jnp.int32, (rows, index_row.shape[1]), 0) == index_row


def split(value):
    high = value.astype(jnp.bfloat16)
    return high, (value - high.astype(jnp.float32)).astype(jnp.bfloat16)


def gather_block(table, index, rows, used):
    row_of = lax.shift_right_arithmetic(index, 7)
    lane_of = index & (LANES - 1)
    got = [jnp.zeros((SUBLANES, LANES), jnp.float32)] * 3
    for r in range(used):
        mask = row_of == r
        for c in range(3):
            at = c * rows + r
            line = jnp.broadcast_to(table[at : at + 1, :], (SUBLANES, LANES))
            value = jnp.take_along_axis(line, lane_of, axis=1, mode="promise_in_bounds")
            got[c] = jnp.where(mask, value, got[c])
    return got


def scatter(values, lane_hot, row_index, rows):
    mask = matches(row_index, rows)
    parts = [split(value) for value in values]
    left = jnp.concatenate(
        [jnp.where(mask, parts[c][s].astype(jnp.float32), 0.0) for s in range(2) for c in range(3)],
        axis=0,
    ).astype(jnp.bfloat16)
    return lax.dot_general(
        left, lane_hot, (((1,), (1,)), ((), ())), preferred_element_type=jnp.float32
    )


def kernel(
    dims,
    given_idx,
    lend_idx,
    owner,
    node,
    mod,
    stiff,
    gap0,
    pen,
    fric,
    slip,
    disp,
    prev,
    load,
    mass,
    out_u,
    out_a,
    idx,
    lane_hot,
    stiff_wide,
    ext,
    ue,
    fe,
    acc_e,
    slot_vals,
    ends,
    pair_vals,
    recv_tab,
    cur,
    old,
    load_tab,
    box_out,
    box_in,
    halo_out,
    halo_in,
    box_send,
    box_recv,
    halo_send,
    halo_recv,
):
    n_py, n, cap, elnode, lent, width = dims
    px, py = lax.axis_index("px"), lax.axis_index("py")
    me = px * n_py + py

    def place(device):
        return {"px": lax.div(device, n_py), "py": lax.rem(device, n_py)}

    barrier = pltpu.get_barrier_semaphore()

    @pl.loop(1, n)
    def _(d):
        pl.semaphore_signal(
            barrier, inc=1, device_id=place(lax.rem(me + d, n)), device_id_type=MESH
        )

    own_rows = cur.shape[0] // 3
    ext_rows = ext.shape[0] // 3
    slots = slot_vals.shape[1]
    slot_rows = recv_tab.shape[0] // 3
    given = given_idx.shape[0]
    wide = stiff_wide.shape[0] // 3
    lend = wide
    pair_chunks = pen.shape[1] // width
    near, far = lend + 1, lend + 1 + pair_chunks

    def set_row(k, row):
        idx[pl.ds(k, 1), :] = row
        lane_hot[k] = jnp.where(matches(row & (LANES - 1), LANES), 1.0, 0.0).astype(jnp.bfloat16)

    def scatter_row(values, k, rows):
        row = lax.shift_right_arithmetic(idx[pl.ds(k, 1), :], 7)
        return scatter(values, lane_hot[k], row, rows)

    @pl.loop(0, given)
    def _(k):
        set_row(k, given_idx[pl.ds(k, 1), :])

    stiff_wide[...] = jnp.zeros_like(stiff_wide)
    for c in range(3):
        for d in range(3):
            stiff_wide[c * wide : c * wide + elnode, d * wide : d * wide + elnode] = stiff[
                c * elnode : (c + 1) * elnode, d * elnode : (d + 1) * elnode
            ]

    before = (
        lax.broadcasted_iota(jnp.int32, (width, width), 0)
        < lax.broadcasted_iota(jnp.int32, (width, width), 1)
    )
    before = jnp.where(before, 1.0, 0.0).astype(jnp.bfloat16)
    carry = jnp.zeros((n, 1), jnp.float32)
    found = jnp.zeros((2 * slots, width), jnp.float32)
    for j in range(owner.shape[0]):
        target = owner[j : j + 1, :]
        mask = matches(target, n)
        hot = jnp.where(mask, 1.0, 0.0)
        earlier = jnp.dot(hot.astype(jnp.bfloat16), before, preferred_element_type=jnp.float32)
        rank = jnp.sum(jnp.where(mask, earlier + carry, 0.0), axis=0, keepdims=True)
        carry = carry + jnp.sum(hot, axis=1, keepdims=True)
        slot = target * cap + rank.astype(jnp.int32)
        mask = matches(lax.div(slot, width), slots)
        number = node[j : j + 1, :] + 1
        left = jnp.concatenate(
            [
                jnp.where(mask, lax.shift_right_arithmetic(number, 6).astype(jnp.float32), 0.0),
                jnp.where(mask, (number & 63).astype(jnp.float32), 0.0),
            ],
            axis=0,
        ).astype(jnp.bfloat16)
        right = jnp.where(matches(lax.rem(slot, width), width), 1.0, 0.0).astype(jnp.bfloat16)
        found = found + lax.dot_general(
            left, right, (((1,), (1,)), ((), ())), preferred_element_type=jnp.float32
        )
    numbers = (found[:slots] * 64.0 + found[slots:]).astype(jnp.int32) - 1
    for q in range(slots):
        set_row(given + q, numbers[q : q + 1, :])

    for c in range(3):
        for r in range(own_rows):
            at, lanes = c * own_rows + r, slice(r * LANES, (r + 1) * LANES)
            cur[at : at + 1, :] = disp[c : c + 1, lanes]
            old[at : at + 1, :] = prev[c : c + 1, lanes]
            load_tab[at : at + 1, :] = load[c : c + 1, lanes]
    ext[...] = jnp.zeros_like(ext)

    def box_copy(i, d):
        other = lax.rem(me + d, n)
        return pltpu.make_async_remote_copy(
            src_ref=box_out.at[i, other],
            dst_ref=box_in.at[i, me],
            send_sem=box_send.at[i],
            recv_sem=box_recv.at[i],
            device_id=place(other),
            device_id_type=MESH,
        )

    def box_start(i):
        @pl.loop(1, n)
        def _(d):
            box_copy(i, d).start()

        box_in[i, me] = box_out[i, me]

    def box_wait(i):
        every = pl.ds(0, n - 1)
        whole = pltpu.make_async_remote_copy(
            src_ref=box_out.at[i, every],
            dst_ref=box_in.at[i, every],
            send_sem=box_send.at[i],
            recv_sem=box_recv.at[i],
            device_id=place(lax.rem(me + 1, n)),
            device_id_type=MESH,
        )
        whole.wait()

    def halo_copies(i):
        copies = []
        for side, step in ((0, n - 1), (1, 1)):
            copies.append(
                pltpu.make_async_remote_copy(
                    src_ref=halo_out.at[i, side],
                    dst_ref=halo_in.at[i, 1 - side],
                    send_sem=halo_send.at[i, side],
                    recv_sem=halo_recv.at[i, 1 - side],
                    device_id=place(lax.rem(me + step, n)),
                    device_id_type=MESH,
                )
            )
        return copies

    def halo_start(i):
        for copy in halo_copies(i):
            copy.start()

    def halo_wait(i):
        for copy in halo_copies(i):
            copy.wait()

    def halo_side(i, side, c):
        inside = me > 0 if side == 0 else me < n - 1
        return jnp.where(inside, halo_in[i, side, c : c + 1, :], 0.0)

    lent_rows = lent // LANES
    blocks = width // LANES

    def gather_rows(table, first, count, rows, used, store):
        @pl.loop(0, count // SUBLANES * blocks, unroll=2)
        def _(i):
            row = pl.multiple_of(lax.div(i, blocks) * SUBLANES, SUBLANES)
            lane = pl.multiple_of(lax.rem(i, blocks) * LANES, LANES)
            index = idx[pl.ds(first + row, SUBLANES), pl.ds(lane, LANES)]
            for c, value in enumerate(gather_block(table, index, rows, used)):
                store(c, pl.ds(row, SUBLANES), pl.ds(lane, LANES), value)

    def slot_store(c, rows, lanes, value):
        slot_vals[c, rows, lanes] = value

    def element_store(c, rows, lanes, value):
        ue[c, rows, lanes] = value

    def end_store(c, rows, lanes, value):
        ends[c, rows, lanes] = value

    for step in range(STEPS):
        going, back = 2 * step, 2 * step + 1
        lending = gather_block(cur, lend_idx[...], own_rows, own_rows)
        for c in range(3):
            for side in range(2):
                for r in range(lent_rows):
                    at = side * lent_rows + r
                    halo_out[going, side, c : c + 1, r * LANES : (r + 1) * LANES] = lending[c][
                        at : at + 1
                    ]
        if step == 0:
            pl.semaphore_wait(barrier, n - 1)
        halo_start(going)

        gather_rows(cur, given, slots, own_rows, own_rows, slot_store)

        for o in range(n):
            r, l = divmod(o * cap, width)
            for c in range(3):
                box_out[going, o, c : c + 1, :] = slot_vals[c, r : r + 1, l : l + cap]
        box_start(going)

        halo_wait(going)
        for c in range(3):
            ext[c * ext_rows : c * ext_rows + own_rows, :] = cur[c * own_rows : (c + 1) * own_rows, :]
            for side in range(2):
                ghosts = halo_side(going, side, c)
                for r in range(lent_rows):
                    at = c * ext_rows + own_rows + side * lent_rows + r
                    ext[at : at + 1, :] = ghosts[:, r * LANES : (r + 1) * LANES]

        gather_rows(ext, 0, wide, ext_rows, own_rows + 2 * lent_rows, element_store)

        box_wait(going)
        for g in range(n):
            r, l = divmod(g * cap, LANES)
            for c in range(3):
                at = c * slot_rows + r
                recv_tab[at : at + 1, l : l + cap] = box_in[going, g, c : c + 1, :]
        gather_rows(recv_tab, lend, SUBLANES, slot_rows, slot_rows, end_store)
        total = jnp.zeros((6 * slot_rows, LANES), jnp.float32)
        for p in range(pair_chunks):
            cols = slice(p * width, (p + 1) * width)
            low = [ends[c, 1 + p : 2 + p, :] for c in range(3)]
            high = [ends[c, 1 + pair_chunks + p : 2 + pair_chunks + p, :] for c in range(3)]
            gap = [gap0[c : c + 1, cols] + high[c] - low[c] for c in range(3)]
            normal = pen[:, cols] * jnp.maximum(-gap[2], 0.0)
            length = jnp.sqrt(gap[0] * gap[0] + gap[1] * gap[1] + 0.01)
            slipping = slip[step : step + 1, cols] == 1
            factor = jnp.where(
                slipping, -fric[:, cols] * normal / length, -0.5 * pen[:, cols]
            )
            force = [factor * gap[0], factor * gap[1], normal]
            total = total + scatter_row(force, far + p, slot_rows)
            total = total - scatter_row(force, near + p, slot_rows)
        pair_vals[...] = total[: 3 * slot_rows] + total[3 * slot_rows :]
        for g in range(n):
            r, l = divmod(g * cap, LANES)
            for c in range(3):
                at = c * slot_rows + r
                box_out[back, g, c : c + 1, :] = pair_vals[at : at + 1, l : l + cap]
        box_start(back)

        fe[...] = (
            jnp.dot(
                stiff_wide[...],
                ue[...].reshape(3 * wide, width),
                precision=lax.Precision.HIGHEST,
                preferred_element_type=jnp.float32,
            )
            * mod[...]
        )
        acc_e[...] = jnp.zeros_like(acc_e)

        some = next(f for f in (9, 3, 1) if elnode % f == 0)

        @pl.loop(0, elnode // some)
        def _(group):
            total = acc_e[...]
            for i in range(some):
                k = group * some + i
                values = [fe[pl.ds(c * wide + k, 1), :] for c in range(3)]
                total = total + scatter_row(values, k, ext_rows)
            acc_e[...] = total

        ext[...] = acc_e[: 3 * ext_rows] + acc_e[3 * ext_rows :]
        for c in range(3):
            for side in range(2):
                for r in range(lent_rows):
                    at = c * ext_rows + own_rows + side * lent_rows + r
                    halo_out[back, side, c : c + 1, r * LANES : (r + 1) * LANES] = ext[at : at + 1, :]
        halo_start(back)

        box_wait(back)
        for o in range(n):
            r, l = divmod(o * cap, width)
            for c in range(3):
                slot_vals[c, r : r + 1, l : l + cap] = box_in[back, o, c : c + 1, :]
        contact = jnp.zeros((6 * own_rows, LANES), jnp.float32)
        for q in range(slots):
            values = [slot_vals[c, q : q + 1, :] for c in range(3)]
            contact = contact + scatter_row(values, given + q, own_rows)

        halo_wait(back)
        values = [
            jnp.concatenate([halo_side(back, 0, c), halo_side(back, 1, c)], axis=1) for c in range(3)
        ]
        total = contact - scatter_row(values, lend, own_rows)
        total = total[: 3 * own_rows] + total[3 * own_rows :]
        for c in range(3):
            rows = slice(c * own_rows, (c + 1) * own_rows)
            internal = ext[c * ext_rows : c * ext_rows + own_rows, :]
            acceleration = (load_tab[rows, :] - internal + total[rows]) / mass[...]
            now = cur[rows, :]
            later = 2.0 * now - old[rows, :] + time_step_sq * acceleration
            old[rows, :] = now
            cur[rows, :] = later
            if step == STEPS - 1:
                for r in range(own_rows):
                    lanes = slice(r * LANES, (r + 1) * LANES)
                    out_u[c : c + 1, lanes] = later[r : r + 1]
                    out_a[c : c + 1, lanes] = acceleration[r : r + 1]


def on_device(
    n_py,
    displacement,
    disp_prev,
    nodal_load,
    nodal_mass,
    modulus,
    stiffness,
    connectivity,
    ghost_send,
    contact_node,
    contact_owner,
    pair_ids,
    gap_start,
    penalty,
    friction,
    slip_state,
):
    n = lax.axis_size(("px", "py"))
    cap = 2 * contact_node.shape[0] // n
    elnode, width = connectivity.shape
    nodes = displacement.shape[1]
    lent = ghost_send.shape[1]
    own_rows = nodes // LANES
    ext_rows = -(-(own_rows + 2 * lent // LANES) // SUBLANES) * SUBLANES
    slots = n * cap // width
    slot_rows = n * cap // LANES
    wide = -(-elnode // SUBLANES) * SUBLANES
    pairs = pair_ids.reshape(-1, width)
    idx = jnp.concatenate(
        [
            jnp.pad(connectivity, ((0, wide - elnode), (0, 0)), constant_values=-1),
            ghost_send.reshape(1, 2 * lent),
            jnp.pad(pairs, ((0, -(1 + pairs.shape[0]) % SUBLANES), (0, 0)), constant_values=-1),
        ],
        axis=0,
    )
    lend_idx = ghost_send.reshape(-1, LANES)
    lend_idx = jnp.pad(lend_idx, ((0, -lend_idx.shape[0] % SUBLANES), (0, 0)), constant_values=-1)
    chunks = idx.shape[0] + slots
    flat = (3 * own_rows, LANES)
    vmem = pl.BlockSpec(memory_space=pltpu.VMEM)
    f32, bf16 = jnp.float32, jnp.bfloat16
    dma = pltpu.SemaphoreType.DMA
    new_u, acc = pl.pallas_call(
        functools.partial(kernel, (n_py, n, cap, elnode, lent, width)),
        out_shape=[jax.ShapeDtypeStruct(displacement.shape, f32)] * 2,
        in_specs=[vmem] * 14,
        out_specs=[vmem] * 2,
        scratch_shapes=[
            pltpu.VMEM((chunks, width), jnp.int32),
            pltpu.VMEM((chunks, LANES, width), bf16),
            pltpu.VMEM((3 * wide, 3 * wide), f32),
            pltpu.VMEM((3 * ext_rows, LANES), f32),
            pltpu.VMEM((3, wide, width), f32),
            pltpu.VMEM((3 * wide, width), f32),
            pltpu.VMEM((6 * ext_rows, LANES), f32),
            pltpu.VMEM((3, slots, width), f32),
            pltpu.VMEM((3, SUBLANES, width), f32),
            pltpu.VMEM((3 * slot_rows, LANES), f32),
            pltpu.VMEM((3 * slot_rows, LANES), f32),
            pltpu.VMEM(flat, f32),
            pltpu.VMEM(flat, f32),
            pltpu.VMEM(flat, f32),
            pltpu.VMEM((2 * STEPS, n, 3, cap), f32),
            pltpu.VMEM((2 * STEPS, n, 3, cap), f32),
            pltpu.VMEM((2 * STEPS, 2, 3, lent), f32),
            pltpu.VMEM((2 * STEPS, 2, 3, lent), f32),
            dma((2 * STEPS,)),
            dma((2 * STEPS,)),
            dma((2 * STEPS, 2)),
            dma((2 * STEPS, 2)),
        ],
        compiler_params=pltpu.CompilerParams(
            collective_id=0, has_side_effects=True, vmem_limit_bytes=48 * 1024 * 1024
        ),
        name="contact_steps",
    )(
        idx,
        lend_idx,
        contact_owner.reshape(-1, width),
        contact_node.reshape(-1, width),
        modulus.reshape(1, -1),
        stiffness,
        gap_start,
        penalty.reshape(1, -1),
        friction.reshape(1, -1),
        slip_state,
        displacement,
        disp_prev,
        nodal_load,
        nodal_mass.reshape(-1, LANES),
    )
    return new_u, acc


def solution(mesh):
    both = ("px", "py")
    row, cols = P(both), P(None, both)
    return jax.shard_map(
        functools.partial(on_device, mesh.shape["py"]),
        mesh=mesh,
        in_specs=(cols, cols, cols, row, row, P(), cols, cols, row, row, cols, cols, row, row, cols),
        out_specs=(cols, cols),
        check_vma=False,
    )
```
